32 devices in a mesh: grp: 2 (over y), row: 4 (over z), col: 2 (over x), sub: 2 (over core).
Axes of the slice: x: 2, y: 2, z: 4, core: 2. Of those that a mesh axis runs over, the one named last changes fastest.
Arguments:
- spectra: bfloat16 [128, 3, 2, 256], P(('grp', 'row', 'col', 'sub')), parts along dimension 0, may hold values from -24 to 24
- valid_mask: int32 [128, 3], P(('grp', 'row', 'col', 'sub')), parts along dimension 0, may hold values 0 or 1
Outputs:
- maxima: float32 [4, 128, 16], P(('col', 'sub'), ('grp', 'row')), parts along dimension 1
The draws below stay inside these ranges and needn't reach their ends.
There are 2 independent parts, one for each index of `grp`. The reference program is written for one: setup_inputs(seed, part) draws one part's arguments, and reference() takes and returns one part's arrays. A program takes and returns all parts, laid end to end along the dimension named above; each array names one. Nothing has to cross between parts.
All inputs are finite; a program needn't handle non-finite values. No bound on the sum of `valid_mask` on one device may be relied on, other than what follows from the above.
Results may differ from the reference program's by a relative error of at most 0.0003.
Values may be sent and summed in bfloat16 or wider, within the bound.
No kernel may reach another device: no remote copies, remote signals or barrier semaphores. Data moves between devices by JAX's collectives and lax.ppermute only.
A program may use at most 64 MiB of HBM per device.

```python
import math
import jax
import jax.numpy as jnp
from jax import lax

SH = 4
BINS = 256
COMP = 3
NSAMP = 2048
FIRST_BIN = 20
MAXLAG = 32
EVENTS = 64
BLOCK = 16
FAMILIES = 4
N_ROW = 4


def draw_spectra(key, part):
    keys = jax.random.split(jax.random.fold_in(key, 17), 5)
    family = jax.random.randint(keys[0], (EVENTS,), 0, FAMILIES)
    offset = jax.random.randint(keys[1], (EVENTS,), -(MAXLAG // 2), MAXLAG // 2 + 1)
    templates = jax.random.normal(keys[2], (FAMILIES, COMP, 2, BINS), jnp.float32)
    chosen = templates[family]
    noise = jax.random.normal(keys[3], (EVENTS, COMP, 2, BINS), jnp.float32)
    scale = jnp.exp(jax.random.uniform(keys[4], (EVENTS,), jnp.float32, math.log(0.5), math.log(2.0)))
    frequency = (FIRST_BIN + jnp.arange(BINS)).astype(jnp.float32)
    angle = 2.0 * math.pi / NSAMP * offset.astype(jnp.float32)[:, None] * frequency[None, :]
    cos_table = jnp.cos(angle)[:, None, :]
    sin_table = jnp.sin(angle)[:, None, :]
    real_part = chosen[:, :, 0, :] * cos_table + chosen[:, :, 1, :] * sin_table
    imag_part = chosen[:, :, 1, :] * cos_table - chosen[:, :, 0, :] * sin_table
    signal = jnp.stack([real_part, imag_part], axis=2)
    result = scale[:, None, None, None] * (0.75 * signal + 0.66 * noise)
    return jnp.clip(result, -24.0, 24.0).astype(jnp.bfloat16)


def touch_ends(values, rng, low, high):
    place = [jax.random.randint(jax.random.fold_in(rng, axis), (), 0, length) for axis, length in enumerate(values.shape)]
    widest = values.shape.index(max(values.shape))
    beside = place[:widest] + [(place[widest] + 1) % values.shape[widest]] + place[widest + 1:]
    return values.at[tuple(place)].set(low).at[tuple(beside)].set(high)


def setup_inputs(seed: int = 0, part: int = 0) -> dict:
    arg_keys = jax.random.split(jax.random.key(seed), 3)
    part_splits = jax.random.split(jax.random.fold_in(arg_keys[2], part), 3)
    return {
        "spectra": draw_spectra(jax.random.fold_in(jax.random.fold_in(arg_keys[2], part), 71), part),
        "valid_mask": touch_ends((jax.random.randint(part_splits[1], (EVENTS, COMP), 0, 4) < 3).astype(jnp.int32), jax.random.fold_in(part_splits[1], 1), 0, 1),
    }


FLOOR = 0.25

def phase_tables():
    lag_values = jnp.arange(-MAXLAG, MAXLAG + 1).astype(jnp.float32)
    frequency = (FIRST_BIN + jnp.arange(BINS)).astype(jnp.float32)
    angle = 2.0 * math.pi / NSAMP * lag_values[:, None] * frequency[None, :]
    return (jnp.cos(angle), jnp.sin(angle))

def masked_of(records, flags):
    return records * flags.astype(jnp.bfloat16)[:, :, None, None]

def energy_of(masked):
    floats = masked.astype(jnp.float32)
    return lax.optimization_barrier(jnp.mean(floats * floats, axis=(2, 3)))

def rotate(masked, cosine, sine):
    floats = masked.astype(jnp.float32)
    real_part = floats[:, None, :, 0, :]
    imag_part = floats[:, None, :, 1, :]
    cos_table = cosine[None, :, None, :]
    sin_table = sine[None, :, None, :]
    new_real = real_part * cos_table - imag_part * sin_table
    new_imag = real_part * sin_table + imag_part * cos_table
    stacked = jnp.stack([new_real, new_imag], axis=3)
    return stacked.reshape(masked.shape[0] * cosine.shape[0], -1)

def pair_values(rotated, row_energy, row_flags, col_masked, col_flags):
    row_count = row_energy.shape[0]
    col_count = col_masked.shape[0]
    bin_count = col_masked.shape[3]
    flat_cols = col_masked.reshape(col_count, -1).astype(jnp.float32)
    products = lax.dot_general(rotated, flat_cols, (((1,), (1,)), ((), ())), precision=lax.Precision.HIGHEST, preferred_element_type=jnp.float32)
    peak_value = lax.optimization_barrier(jnp.max(products.reshape(row_count, -1, col_count), axis=1)) / (2.0 * bin_count)
    col_energy = energy_of(col_masked)
    shared_row = lax.optimization_barrier(jnp.sum((row_energy * row_flags)[:, None, :] * col_flags[None, :, :], axis=2))
    shared_col = lax.optimization_barrier(jnp.sum(row_flags[:, None, :] * (col_energy * col_flags)[None, :, :], axis=2))
    return peak_value / jnp.sqrt(jnp.maximum(shared_row * shared_col, FLOOR))

def reference(spectra, valid_mask):
    cosine, sine = phase_tables()
    masked = masked_of(spectra, valid_mask)
    energy = energy_of(masked)
    flags = valid_mask.astype(jnp.float32)

    def one_block(inputs):
        block_masked, block_energy, block_flags = inputs
        rotated = rotate(block_masked, cosine, sine)
        return pair_values(rotated, block_energy, block_flags, masked, flags)
    full_grid = lax.map(one_block, (masked.reshape(N_ROW, BLOCK, COMP, 2, BINS), energy.reshape(N_ROW, BLOCK, COMP), flags.reshape(N_ROW, BLOCK, COMP)))
    full_grid = full_grid.reshape(EVENTS, EVENTS)
    groups = BLOCK // SH
    return full_grid.reshape(EVENTS, N_ROW, groups, SH).transpose(2, 0, 1, 3).reshape(groups, EVENTS, N_ROW * SH)
```

```python
import functools
import math

import jax
import jax.numpy as jnp
import numpy as np
from jax import lax
from jax.experimental import pallas as pl
from jax.experimental.pallas import tpu as pltpu
from jax.sharding import PartitionSpec as P

BINS = 256
COMP = 3
NSAMP = 2048
FIRST_BIN = 20
MAXLAG = 32
FLOOR = 0.25
PLANES = 3 * COMP
LAGS = 40


def phase_tables():
    lag = np.arange(LAGS)
    lag = np.where(lag <= MAXLAG, lag, 0)
    angle = 2.0 * math.pi / NSAMP * lag[:, None] * (FIRST_BIN + np.arange(BINS))[None, :]
    both = []
    for table in (np.cos(angle), np.sin(angle)):
        high = table.astype(jnp.bfloat16)
        low = (table - high.astype(np.float64)).astype(jnp.bfloat16)
        both.append(np.concatenate([high, low], axis=0))
    return np.stack(both)


def pack_kernel(spectra_ref, mask_ref, out_ref):
    floats = spectra_ref[...].astype(jnp.float32)
    flags = mask_ref[...].astype(jnp.float32)
    for c in range(COMP):
        flag = jnp.broadcast_to(flags[:, c : c + 1], (flags.shape[0], BINS))
        out_ref[2 * c] = (floats[:, c, 0, :] * flag).astype(jnp.bfloat16)
        out_ref[2 * c + 1] = (floats[:, c, 1, :] * flag).astype(jnp.bfloat16)
        out_ref[2 * COMP + c] = flag.astype(jnp.bfloat16)


def pack(spectra, valid_mask):
    rows = spectra.shape[0]
    return pl.pallas_call(
        pack_kernel,
        out_shape=jax.ShapeDtypeStruct((PLANES, rows, BINS), jnp.bfloat16),
        in_specs=[pl.BlockSpec(memory_space=pltpu.VMEM)] * 2,
        out_specs=pl.BlockSpec(memory_space=pltpu.VMEM),
        compiler_params=pltpu.CompilerParams(vmem_limit_bytes=1 << 20),
        name="pack",
    )(spectra, valid_mask)


def split(value):
    high = value.astype(jnp.bfloat16)
    return high, (value - high.astype(jnp.float32)).astype(jnp.bfloat16)


def dot_nt(left, right):
    return lax.dot_general(left, right, (((1,), (1,)), ((), ())), preferred_element_type=jnp.float32)


def shared_sums(left, right):
    total = None
    for one, other in zip(left, right):
        for i in range(len(one)):
            for j in range(len(other)):
                term = dot_nt(one[i], other[j])
                total = term if total is None else total + term
    return total / (2.0 * BINS)


def pair_kernel(n_cs, n_row, *refs):
    own_ref = refs[0]
    cs_refs = refs[1:n_cs]
    down_refs = refs[n_cs : n_cs + n_row - 1]
    up_refs = refs[n_cs + n_row - 1 : n_cs + 2 * n_row - 2]
    table_ref, out_ref, row_scr, col_scr, x_scr, y_scr = refs[n_cs + 2 * n_row - 2 :]
    shard = own_ref.shape[1]
    me_cs = lax.axis_index("col") * lax.axis_size("sub") + lax.axis_index("sub")
    me_row = lax.axis_index("row")
    own = own_ref[...].astype(jnp.float32)
    row_scr[me_cs] = own
    col_scr[me_row] = own
    for k in range(1, n_cs):
        row_scr[me_cs ^ k] = cs_refs[k - 1][...].astype(jnp.float32)
    for k in range(1, n_row):
        down = down_refs[k - 1][...].astype(jnp.float32)
        up = up_refs[k - 1][...].astype(jnp.float32)
        other = me_row ^ k
        col_scr[other] = jnp.where(other > me_row, down, up)
    rows, cols = n_cs * shard, n_row * shard
    per = 128 // cols
    col_planes = [jnp.concatenate([col_scr[j, q] for j in range(n_row)], axis=0) for q in range(PLANES)]
    for a in range(rows):
        x, y = None, None
        for c in range(COMP):
            re = row_scr[a // shard, 2 * c, pl.ds(a % shard, 1), :]
            im = row_scr[a // shard, 2 * c + 1, pl.ds(a % shard, 1), :]
            xc = re * col_planes[2 * c] + im * col_planes[2 * c + 1]
            yc = im * col_planes[2 * c] - re * col_planes[2 * c + 1]
            x = xc if x is None else x + xc
            y = yc if y is None else y + yc
        place = (a // per * per + (per - a % per) % per) * cols
        x_scr[pl.ds(place, cols), :] = x
        y_scr[pl.ds(place, cols), :] = y
    halves = []
    for scr, i in ((x_scr, 0), (y_scr, 1)):
        high, low = split(scr[...])
        first = dot_nt(table_ref[i], high)
        second = dot_nt(table_ref[i, :LAGS], low)
        halves.append(first[:LAGS] + first[LAGS:] + second)
    best = jnp.max(halves[0] + jnp.abs(halves[1]), axis=0, keepdims=True)
    pieces = []
    for h in range(rows // per):
        piece = jnp.broadcast_to(best[:, 128 * h : 128 * (h + 1)], (per, 128))
        pieces.append(pltpu.roll(piece, 0, 1, stride=cols, stride_axis=0)[:, :cols])
    peak = jnp.concatenate(pieces, axis=0) / (2.0 * BINS)
    row_planes = [jnp.concatenate([row_scr[j, q] for j in range(n_cs)], axis=0) for q in range(PLANES)]

    def energy(planes):
        return [split(planes[2 * c] * planes[2 * c] + planes[2 * c + 1] * planes[2 * c + 1]) for c in range(COMP)]

    def flags(planes):
        return [(planes[2 * COMP + c].astype(jnp.bfloat16),) for c in range(COMP)]

    shared_row = shared_sums(energy(row_planes), flags(col_planes))
    shared_col = shared_sums(flags(row_planes), energy(col_planes))
    out_ref[0] = peak / jnp.sqrt(jnp.maximum(shared_row * shared_col, FLOOR))


def shards_small(spectra, valid_mask):
    n_row = lax.axis_size("row")
    n_cs = lax.axis_size("col") * lax.axis_size("sub")
    shard = spectra.shape[0]
    own = pack(spectra, valid_mask)
    cs_axes = ("col", "sub")
    cs, down, up = {}, {}, {}
    for k in (3, 2, 1):
        up[k] = lax.ppermute(own, "row", [(i, i ^ k) for i in range(n_row) if i < i ^ k])
    for k in (3, 2):
        cs[k] = lax.ppermute(own, cs_axes, [(i, i ^ k) for i in range(n_cs)])
    for k in (1, 2, 3):
        down[k] = lax.ppermute(own, "row", [(i, i ^ k) for i in range(n_row) if i > i ^ k])
    cs[1] = lax.ppermute(own, cs_axes, [(i, i ^ 1) for i in range(n_cs)])
    cs, down, up = ([d[k] for k in (1, 2, 3)] for d in (cs, down, up))
    rows, cols = n_cs * shard, n_row * shard
    return pl.pallas_call(
        functools.partial(pair_kernel, n_cs, n_row),
        out_shape=jax.ShapeDtypeStruct((1, rows, cols), jnp.float32),
        scratch_shapes=[
            pltpu.VMEM((n_cs, PLANES, shard, BINS), jnp.float32),
            pltpu.VMEM((n_row, PLANES, shard, BINS), jnp.float32),
            pltpu.VMEM((rows * cols, BINS), jnp.float32),
            pltpu.VMEM((rows * cols, BINS), jnp.float32),
        ],
        in_specs=[pl.BlockSpec(memory_space=pltpu.VMEM)] * (n_cs + 2 * n_row - 1),
        out_specs=pl.BlockSpec(memory_space=pltpu.VMEM),
        compiler_params=pltpu.CompilerParams(vmem_limit_bytes=8 << 20),
        name="pairs",
    )(own, *cs, *down, *up, jnp.asarray(phase_tables()))


def shards_large(spectra, valid_mask):
    def planes(axes):
        records = lax.all_gather(spectra, axes, axis=0, tiled=True)
        flags = lax.all_gather(valid_mask, axes, axis=0, tiled=True)
        masked = (records * flags.astype(jnp.bfloat16)[:, :, None, None]).astype(jnp.float32)
        return masked, jnp.mean(masked * masked, axis=(2, 3)), flags.astype(jnp.float32)

    row, row_energy, row_flags = planes(("col", "sub"))
    col, col_energy, col_flags = planes("row")
    table = phase_tables().astype(np.float32)
    cosine, sine = table[:, : MAXLAG + 1] + table[:, LAGS : LAGS + MAXLAG + 1]

    def one(args):
        row_one, energy_one, flags_one = args
        re, im = row_one[None, :, 0], row_one[None, :, 1]
        x = jnp.sum(re * col[:, :, 0] + im * col[:, :, 1], axis=1)
        y = jnp.sum(im * col[:, :, 0] - re * col[:, :, 1], axis=1)
        even = jnp.dot(x, cosine.T, precision=lax.Precision.HIGHEST)
        odd = jnp.dot(y, sine.T, precision=lax.Precision.HIGHEST)
        peak = jnp.max(even + jnp.abs(odd), axis=1) / (2.0 * BINS)
        shared_row = jnp.sum((energy_one * flags_one)[None] * col_flags, axis=1)
        shared_col = jnp.sum(flags_one[None] * (col_energy * col_flags), axis=1)
        return peak / jnp.sqrt(jnp.maximum(shared_row * shared_col, FLOOR))

    return lax.map(one, (row, row_energy, row_flags))[None]


def solution(mesh):
    small = mesh.shape["row"] == 4 and mesh.shape["col"] == 2 and mesh.shape["sub"] == 2
    in_specs = (
        P(("grp", "row", "col", "sub"), None, None, None),
        P(("grp", "row", "col", "sub"), None),
    )
    out_specs = P(("col", "sub"), ("grp", "row"), None)
    return jax.shard_map(
        shards_small if small else shards_large, mesh=mesh, in_specs=in_specs, out_specs=out_specs, check_vma=False
    )
```

```python
import functools
import math

import jax
import jax.numpy as jnp
import numpy as np
from jax import lax
from jax.experimental import pallas as pl
from jax.experimental.pallas import tpu as pltpu
from jax.sharding import PartitionSpec as P

BINS = 256
COMP = 3
NSAMP = 2048
FIRST_BIN = 20
MAXLAG = 32
FLOOR = 0.25
CS = ("col", "sub")
ORDER = (("row", 3), ("row", 2), ("row", 1), (CS, 3), (CS, 2), (CS, 1))
PLANES = 3 * COMP
LAGS = 40


def phase_tables():
    lag = np.arange(LAGS)
    lag = np.where(lag <= MAXLAG, lag, 0)
    angle = 2.0 * math.pi / NSAMP * lag[:, None] * (FIRST_BIN + np.arange(BINS))[None, :]
    both = []
    for table in (np.cos(angle), np.sin(angle)):
        high = table.astype(jnp.bfloat16)
        low = (table - high.astype(np.float64)).astype(jnp.bfloat16)
        both.append(np.concatenate([high, low], axis=0))
    return np.stack(both)


def in_hbm(value):
    return pltpu.with_memory_space_constraint(value, pltpu.HBM)


def pack_kernel(spectra_hbm, mask_hbm, table_hbm, out_ref, table_ref, spectra_ref, mask_ref, sem):
    copies = [
        pltpu.make_async_copy(spectra_hbm, spectra_ref, sem.at[0]),
        pltpu.make_async_copy(mask_hbm, mask_ref, sem.at[1]),
        pltpu.make_async_copy(table_hbm, table_ref, sem.at[2]),
    ]
    for copy in copies:
        copy.start()
    copies[0].wait()
    copies[1].wait()
    floats = spectra_ref[...].astype(jnp.float32)
    flags = mask_ref[...].astype(jnp.float32)
    for c in range(COMP):
        flag = jnp.broadcast_to(flags[:, c : c + 1], (flags.shape[0], BINS))
        out_ref[2 * c] = (floats[:, c, 0, :] * flag).astype(jnp.bfloat16)
        out_ref[2 * c + 1] = (floats[:, c, 1, :] * flag).astype(jnp.bfloat16)
        out_ref[2 * COMP + c] = flag.astype(jnp.bfloat16)
    copies[2].wait()


def pack(spectra, valid_mask, table):
    shape = (PLANES, spectra.shape[0], BINS)
    return pl.pallas_call(
        pack_kernel,
        out_shape=(jax.ShapeDtypeStruct(shape, jnp.bfloat16), jax.ShapeDtypeStruct(table.shape, table.dtype)),
        in_specs=[pl.BlockSpec(memory_space=pltpu.HBM)] * 3,
        out_specs=(pl.BlockSpec(memory_space=pltpu.VMEM), pl.BlockSpec(memory_space=pltpu.VMEM)),
        scratch_shapes=[
            pltpu.VMEM(spectra.shape, spectra.dtype),
            pltpu.VMEM(valid_mask.shape, valid_mask.dtype),
            pltpu.SemaphoreType.DMA((3,)),
        ],
        compiler_params=pltpu.CompilerParams(vmem_limit_bytes=1 << 20),
        name="pack",
    )(in_hbm(spectra), in_hbm(valid_mask), in_hbm(table))


def split(value):
    high = value.astype(jnp.bfloat16)
    return high, (value - high.astype(jnp.float32)).astype(jnp.bfloat16)


def dot_nt(left, right):
    return lax.dot_general(left, right, (((1,), (1,)), ((), ())), preferred_element_type=jnp.float32)


def shared_sums(left, right):
    total = None
    for one, other in zip(left, right):
        for i in range(len(one)):
            for j in range(len(other)):
                term = dot_nt(one[i], other[j])
                total = term if total is None else total + term
    return total / (2.0 * BINS)


def pair_kernel(n_cs, n_row, *refs):
    own_ref = refs[0]
    moved = dict(zip(reversed(ORDER), refs[1:]))
    table_ref, out_ref, row_scr, col_scr, x_scr, y_scr = refs[n_cs + n_row - 1 :]
    shard = own_ref.shape[1]
    me_cs = lax.axis_index("col") * lax.axis_size("sub") + lax.axis_index("sub")
    me_row = lax.axis_index("row")
    own = own_ref[...].astype(jnp.float32)
    row_scr[me_cs] = own
    col_scr[me_row] = own
    for k in range(1, n_cs):
        row_scr[me_cs ^ k] = moved[CS, k][...].astype(jnp.float32)
    for k in range(1, n_row):
        col_scr[me_row ^ k] = moved["row", k][...].astype(jnp.float32)
    rows, cols = n_cs * shard, n_row * shard
    per = 128 // cols
    col_planes = [jnp.concatenate([col_scr[j, q] for j in range(n_row)], axis=0) for q in range(PLANES)]
    for a in range(rows):
        x, y = None, None
        for c in range(COMP):
            re = row_scr[a // shard, 2 * c, pl.ds(a % shard, 1), :]
            im = row_scr[a // shard, 2 * c + 1, pl.ds(a % shard, 1), :]
            xc = re * col_planes[2 * c] + im * col_planes[2 * c + 1]
            yc = im * col_planes[2 * c] - re * col_planes[2 * c + 1]
            x = xc if x is None else x + xc
            y = yc if y is None else y + yc
        place = (a // per * per + (per - a % per) % per) * cols
        x_scr[pl.ds(place, cols), :] = x
        y_scr[pl.ds(place, cols), :] = y
    halves = []
    for scr, i in ((x_scr, 0), (y_scr, 1)):
        high, low = split(scr[...])
        first = dot_nt(table_ref[i], high)
        second = dot_nt(table_ref[i, :LAGS], low)
        halves.append(first[:LAGS] + first[LAGS:] + second)
    best = jnp.max(halves[0] + jnp.abs(halves[1]), axis=0, keepdims=True)
    pieces = []
    for h in range(rows // per):
        piece = jnp.broadcast_to(best[:, 128 * h : 128 * (h + 1)], (per, 128))
        pieces.append(pltpu.roll(piece, 0, 1, stride=cols, stride_axis=0)[:, :cols])
    peak = jnp.concatenate(pieces, axis=0) / (2.0 * BINS)
    row_planes = [jnp.concatenate([row_scr[j, q] for j in range(n_cs)], axis=0) for q in range(PLANES)]

    def energy(planes):
        return [split(planes[2 * c] * planes[2 * c] + planes[2 * c + 1] * planes[2 * c + 1]) for c in range(COMP)]

    def flags(planes):
        return [(planes[2 * COMP + c].astype(jnp.bfloat16),) for c in range(COMP)]

    shared_row = shared_sums(energy(row_planes), flags(col_planes))
    shared_col = shared_sums(flags(row_planes), energy(col_planes))
    out_ref[0] = peak / jnp.sqrt(jnp.maximum(shared_row * shared_col, FLOOR))


def shards_small(spectra, valid_mask):
    n_row = lax.axis_size("row")
    n_cs = lax.axis_size("col") * lax.axis_size("sub")
    shard = spectra.shape[0]
    own, table = pack(spectra, valid_mask, jnp.asarray(phase_tables()))
    moved = {}
    for axes, k in ORDER:
        size = n_row if axes == "row" else n_cs
        moved[axes, k] = lax.ppermute(own, axes, [(i, i ^ k) for i in range(size)])
    others = [moved[key] for key in reversed(ORDER)]
    rows, cols = n_cs * shard, n_row * shard
    return pl.pallas_call(
        functools.partial(pair_kernel, n_cs, n_row),
        out_shape=jax.ShapeDtypeStruct((1, rows, cols), jnp.float32),
        scratch_shapes=[
            pltpu.VMEM((n_cs, PLANES, shard, BINS), jnp.float32),
            pltpu.VMEM((n_row, PLANES, shard, BINS), jnp.float32),
            pltpu.VMEM((rows * cols, BINS), jnp.float32),
            pltpu.VMEM((rows * cols, BINS), jnp.float32),
        ],
        in_specs=[pl.BlockSpec(memory_space=pltpu.VMEM)] * (n_cs + n_row),
        out_specs=pl.BlockSpec(memory_space=pltpu.VMEM),
        compiler_params=pltpu.CompilerParams(vmem_limit_bytes=8 << 20),
        name="pairs",
    )(own, *others, table)


def shards_large(spectra, valid_mask):
    def planes(axes):
        records = lax.all_gather(spectra, axes, axis=0, tiled=True)
        flags = lax.all_gather(valid_mask, axes, axis=0, tiled=True)
        masked = (records * flags.astype(jnp.bfloat16)[:, :, None, None]).astype(jnp.float32)
        return masked, jnp.mean(masked * masked, axis=(2, 3)), flags.astype(jnp.float32)

    row, row_energy, row_flags = planes(("col", "sub"))
    col, col_energy, col_flags = planes("row")
    table = phase_tables().astype(np.float32)
    cosine, sine = table[:, : MAXLAG + 1] + table[:, LAGS : LAGS + MAXLAG + 1]

    def one(args):
        row_one, energy_one, flags_one = args
        re, im = row_one[None, :, 0], row_one[None, :, 1]
        x = jnp.sum(re * col[:, :, 0] + im * col[:, :, 1], axis=1)
        y = jnp.sum(im * col[:, :, 0] - re * col[:, :, 1], axis=1)
        even = jnp.dot(x, cosine.T, precision=lax.Precision.HIGHEST)
        odd = jnp.dot(y, sine.T, precision=lax.Precision.HIGHEST)
        peak = jnp.max(even + jnp.abs(odd), axis=1) / (2.0 * BINS)
        shared_row = jnp.sum((energy_one * flags_one)[None] * col_flags, axis=1)
        shared_col = jnp.sum(flags_one[None] * (col_energy * col_flags), axis=1)
        return peak / jnp.sqrt(jnp.maximum(shared_row * shared_col, FLOOR))

    return lax.map(one, (row, row_energy, row_flags))[None]


def solution(mesh):
    small = mesh.shape["row"] == 4 and mesh.shape["col"] == 2 and mesh.shape["sub"] == 2
    in_specs = (
        P(("grp", "row", "col", "sub"), None, None, None),
        P(("grp", "row", "col", "sub"), None),
    )
    out_specs = P(("col", "sub"), ("grp", "row"), None)
    return jax.shard_map(
        shards_small if small else shards_large, mesh=mesh, in_specs=in_specs, out_specs=out_specs, check_vma=False
    )
```

```python
import math

import jax
import jax.numpy as jnp
import numpy as np
from jax import lax
from jax.experimental import pallas as pl
from jax.experimental.pallas import tpu as pltpu
from jax.sharding import PartitionSpec as P

BINS = 256
COMP = 3
NSAMP = 2048
FIRST_BIN = 20
MAXLAG = 32
FLOOR = 0.25
N_PART = 16
LEG_A = (3, 5, 0, 11, 6, 8, 10, 15, 13, 4, 14, 2, 9, 1, 12, 7)
LEG_B = (9, 13, 6, 15, 12, 0, 4, 3, 11, 1, 8, 7, 14, 5, 10, 2)
PLANES = 3 * COMP
LAGS = 40


def phase_tables():
    lag = np.arange(LAGS)
    lag = np.where(lag <= MAXLAG, lag, 0)
    angle = 2.0 * math.pi / NSAMP * lag[:, None] * (FIRST_BIN + np.arange(BINS))[None, :]
    both = []
    for table in (np.cos(angle), np.sin(angle)):
        high = table.astype(jnp.bfloat16)
        low = (table - high.astype(np.float64)).astype(jnp.bfloat16)
        both.append(np.concatenate([high, low], axis=0))
    return np.stack(both)


def in_hbm(value):
    return pltpu.with_memory_space_constraint(value, pltpu.HBM)


def pack_into(out_ref, records, flags):
    floats = records.astype(jnp.float32)
    flags = flags.astype(jnp.float32)
    for c in range(COMP):
        flag = jnp.broadcast_to(flags[:, c : c + 1], (flags.shape[0], BINS))
        out_ref[2 * c] = (floats[:, c, 0, :] * flag).astype(jnp.bfloat16)
        out_ref[2 * c + 1] = (floats[:, c, 1, :] * flag).astype(jnp.bfloat16)
        out_ref[2 * COMP + c] = flag.astype(jnp.bfloat16)


def pack_own_kernel(spectra_hbm, mask_hbm, table_hbm, out_ref, table_ref, spectra_ref, mask_ref, sem):
    copies = [
        pltpu.make_async_copy(spectra_hbm, spectra_ref, sem.at[0]),
        pltpu.make_async_copy(mask_hbm, mask_ref, sem.at[1]),
        pltpu.make_async_copy(table_hbm, table_ref, sem.at[2]),
    ]
    for copy in copies:
        copy.start()
    for copy in copies:
        copy.wait()
    pack_into(out_ref, spectra_ref[...], mask_ref[...])


def pack_own(spectra, valid_mask, table):
    shape = (PLANES, spectra.shape[0], BINS)
    return pl.pallas_call(
        pack_own_kernel,
        out_shape=(jax.ShapeDtypeStruct(shape, jnp.bfloat16), jax.ShapeDtypeStruct(table.shape, table.dtype)),
        in_specs=[pl.BlockSpec(memory_space=pltpu.HBM)] * 3,
        out_specs=(pl.BlockSpec(memory_space=pltpu.VMEM), pl.BlockSpec(memory_space=pltpu.VMEM)),
        scratch_shapes=[
            pltpu.VMEM(spectra.shape, spectra.dtype),
            pltpu.VMEM(valid_mask.shape, valid_mask.dtype),
            pltpu.SemaphoreType.DMA((3,)),
        ],
        compiler_params=pltpu.CompilerParams(vmem_limit_bytes=1 << 20),
        name="pack_own",
    )(in_hbm(spectra), in_hbm(valid_mask), in_hbm(table))


def pack_two_kernel(own_ref, spectra_ref, mask_ref, out_ref):
    me = lax.axis_index("sub")
    out_ref[me] = own_ref[...]
    pack_into(out_ref.at[1 - me], spectra_ref[...], mask_ref[...])


def pack_two(own, spectra, valid_mask):
    return pl.pallas_call(
        pack_two_kernel,
        out_shape=jax.ShapeDtypeStruct((2, *own.shape), own.dtype),
        in_specs=[pl.BlockSpec(memory_space=pltpu.VMEM)] * 3,
        out_specs=pl.BlockSpec(memory_space=pltpu.VMEM),
        compiler_params=pltpu.CompilerParams(vmem_limit_bytes=1 << 20),
        name="pack_two",
    )(own, spectra, valid_mask)


def split(value):
    high = value.astype(jnp.bfloat16)
    return high, (value - high.astype(jnp.float32)).astype(jnp.bfloat16)


def dot_nt(left, right):
    return lax.dot_general(left, right, (((1,), (1,)), ((), ())), preferred_element_type=jnp.float32)


def shared_sums(left, right):
    total = None
    for one, other in zip(left, right):
        for i in range(len(one)):
            for j in range(len(other)):
                term = dot_nt(one[i], other[j])
                total = term if total is None else total + term
    return total / (2.0 * BINS)


def pair_kernel(chip_ref, *refs):
    moved_refs, (table_ref, out_ref, scr, x_scr, y_scr) = refs[:4], refs[4:]
    n_cs = n_row = 4
    shard = scr.shape[2]
    sub = lax.axis_index("sub")
    me_cs = lax.axis_index("col") * 2 + sub
    me_row = lax.axis_index("row")
    me = me_row * 4 + me_cs
    own = chip_ref[sub].astype(jnp.float32)
    scr[me_row] = own
    scr[4 + me_cs] = own
    scr[4 + (me_cs ^ 1)] = chip_ref[1 - sub].astype(jnp.float32)
    codes = arrival_codes()
    for j in range(4):
        code = sum(jnp.where(me == i, codes[i][j], 0) for i in range(N_PART))
        for t in range(2):
            scr[(code >> (4 * t)) & 15] = moved_refs[j][t].astype(jnp.float32)
    col_scr, row_scr = scr.at[:4], scr.at[4:8]
    rows, cols = n_cs * shard, n_row * shard
    per = 128 // cols
    col_planes = [jnp.concatenate([col_scr[j, q] for j in range(n_row)], axis=0) for q in range(PLANES)]
    for a in range(rows):
        x, y = None, None
        for c in range(COMP):
            re = row_scr[a // shard, 2 * c, pl.ds(a % shard, 1), :]
            im = row_scr[a // shard, 2 * c + 1, pl.ds(a % shard, 1), :]
            xc = re * col_planes[2 * c] + im * col_planes[2 * c + 1]
            yc = im * col_planes[2 * c] - re * col_planes[2 * c + 1]
            x = xc if x is None else x + xc
            y = yc if y is None else y + yc
        place = (a // per * per + (per - a % per) % per) * cols
        x_scr[pl.ds(place, cols), :] = x
        y_scr[pl.ds(place, cols), :] = y
    halves = []
    for scr, i in ((x_scr, 0), (y_scr, 1)):
        high, low = split(scr[...])
        first = dot_nt(table_ref[i], high)
        second = dot_nt(table_ref[i, :LAGS], low)
        halves.append(first[:LAGS] + first[LAGS:] + second)
    best = jnp.max(halves[0] + jnp.abs(halves[1]), axis=0, keepdims=True)
    pieces = []
    for h in range(rows // per):
        piece = jnp.broadcast_to(best[:, 128 * h : 128 * (h + 1)], (per, 128))
        pieces.append(pltpu.roll(piece, 0, 1, stride=cols, stride_axis=0)[:, :cols])
    peak = jnp.concatenate(pieces, axis=0) / (2.0 * BINS)
    row_planes = [jnp.concatenate([row_scr[j, q] for j in range(n_cs)], axis=0) for q in range(PLANES)]

    def energy(planes):
        return [split(planes[2 * c] * planes[2 * c] + planes[2 * c + 1] * planes[2 * c + 1]) for c in range(COMP)]

    def flags(planes):
        return [(planes[2 * COMP + c].astype(jnp.bfloat16),) for c in range(COMP)]

    shared_row = shared_sums(energy(row_planes), flags(col_planes))
    shared_col = shared_sums(flags(row_planes), energy(col_planes))
    out_ref[0] = peak / jnp.sqrt(jnp.maximum(shared_row * shared_col, FLOOR))


def arrival_codes():
    from_chip = []
    for legs in (LEG_A, LEG_B):
        source = {target: i for i, target in enumerate(legs)}
        from_chip.append([source[i] // 2 for i in range(N_PART)])
    codes = []
    for i in range(N_PART):
        arrivals = [from_chip[1][i], from_chip[0][i], from_chip[1][i ^ 1], from_chip[0][i ^ 1]]
        one = []
        for chip in arrivals:
            slots = []
            for t in range(2):
                if chip // 2 == i // 4:
                    slots.append(4 + (chip % 2) * 2 + t)
                else:
                    slots.append(chip // 2 if t == i % 2 else 8)
            one.append(slots[0] + 16 * slots[1])
        codes.append(one)
    return codes


def swap(value):
    return lax.ppermute(value, "sub", [(0, 1), (1, 0)])


def leg(value, targets):
    return lax.ppermute(value, ("row", "col", "sub"), list(enumerate(targets)))


def shards_small(spectra, valid_mask):
    shard = spectra.shape[0]
    sub_spectra, sub_mask = swap(spectra), swap(valid_mask)
    own, table = pack_own(spectra, valid_mask, jnp.asarray(phase_tables()))
    chip = pack_two(own, sub_spectra, sub_mask)
    leg_a, leg_b = leg(chip, LEG_A), leg(chip, LEG_B)
    swap_a, swap_b = swap(leg_a), swap(leg_b)
    rows = cols = 4 * shard
    return pl.pallas_call(
        pair_kernel,
        out_shape=jax.ShapeDtypeStruct((1, rows, cols), jnp.float32),
        scratch_shapes=[
            pltpu.VMEM((9, PLANES, shard, BINS), jnp.float32),
            pltpu.VMEM((rows * cols, BINS), jnp.float32),
            pltpu.VMEM((rows * cols, BINS), jnp.float32),
        ],
        in_specs=[pl.BlockSpec(memory_space=pltpu.VMEM)] * 6,
        out_specs=pl.BlockSpec(memory_space=pltpu.VMEM),
        compiler_params=pltpu.CompilerParams(vmem_limit_bytes=8 << 20),
        name="pairs",
    )(chip, leg_b, leg_a, swap_b, swap_a, table)


def shards_large(spectra, valid_mask):
    def planes(axes):
        records = lax.all_gather(spectra, axes, axis=0, tiled=True)
        flags = lax.all_gather(valid_mask, axes, axis=0, tiled=True)
        masked = (records * flags.astype(jnp.bfloat16)[:, :, None, None]).astype(jnp.float32)
        return masked, jnp.mean(masked * masked, axis=(2, 3)), flags.astype(jnp.float32)

    row, row_energy, row_flags = planes(("col", "sub"))
    col, col_energy, col_flags = planes("row")
    table = phase_tables().astype(np.float32)
    cosine, sine = table[:, : MAXLAG + 1] + table[:, LAGS : LAGS + MAXLAG + 1]

    def one(args):
        row_one, energy_one, flags_one = args
        re, im = row_one[None, :, 0], row_one[None, :, 1]
        x = jnp.sum(re * col[:, :, 0] + im * col[:, :, 1], axis=1)
        y = jnp.sum(im * col[:, :, 0] - re * col[:, :, 1], axis=1)
        even = jnp.dot(x, cosine.T, precision=lax.Precision.HIGHEST)
        odd = jnp.dot(y, sine.T, precision=lax.Precision.HIGHEST)
        peak = jnp.max(even + jnp.abs(odd), axis=1) / (2.0 * BINS)
        shared_row = jnp.sum((energy_one * flags_one)[None] * col_flags, axis=1)
        shared_col = jnp.sum(flags_one[None] * (col_energy * col_flags), axis=1)
        return peak / jnp.sqrt(jnp.maximum(shared_row * shared_col, FLOOR))

    return lax.map(one, (row, row_energy, row_flags))[None]


def solution(mesh):
    small = mesh.shape["row"] == 4 and mesh.shape["col"] == 2 and mesh.shape["sub"] == 2
    in_specs = (
        P(("grp", "row", "col", "sub"), None, None, None),
        P(("grp", "row", "col", "sub"), None),
    )
    out_specs = P(("col", "sub"), ("grp", "row"), None)
    return jax.shard_map(
        shards_small if small else shards_large, mesh=mesh, in_specs=in_specs, out_specs=out_specs, check_vma=False
    )
```

```python
import math

import jax
import jax.numpy as jnp
import numpy as np
from jax import lax
from jax.experimental import pallas as pl
from jax.experimental.pallas import tpu as pltpu
from jax.sharding import PartitionSpec as P

BINS = 256
COMP = 3
NSAMP = 2048
FIRST_BIN = 20
MAXLAG = 32
FLOOR = 0.25
N_PART = 16
LEG_A = (3, 5, 0, 11, 6, 8, 10, 15, 13, 4, 14, 2, 9, 1, 12, 7)
LEG_B = (9, 13, 6, 15, 12, 0, 4, 3, 11, 1, 8, 7, 14, 5, 10, 2)
PLANES = 2 * COMP + 1
LAGS = 40


def phase_tables():
    lag = np.arange(LAGS)
    lag = np.where(lag <= MAXLAG, lag, 0)
    angle = 2.0 * math.pi / NSAMP * lag[:, None] * (FIRST_BIN + np.arange(BINS))[None, :]
    both = []
    for table in (np.cos(angle), np.sin(angle)):
        high = table.astype(jnp.bfloat16)
        low = (table - high.astype(np.float64)).astype(jnp.bfloat16)
        both.append(np.concatenate([high, low], axis=0))
    return np.stack(both)


def in_hbm(value):
    return pltpu.with_memory_space_constraint(value, pltpu.HBM)


def pack_into(out_ref, records, flags):
    floats = records.astype(jnp.float32)
    flags = flags.astype(jnp.float32)
    lane = lax.broadcasted_iota(jnp.int32, (flags.shape[0], BINS), 1)
    packed = jnp.zeros(lane.shape, jnp.float32)
    for c in range(COMP):
        flag = jnp.broadcast_to(flags[:, c : c + 1], lane.shape)
        out_ref[2 * c] = (floats[:, c, 0, :] * flag).astype(jnp.bfloat16)
        out_ref[2 * c + 1] = (floats[:, c, 1, :] * flag).astype(jnp.bfloat16)
        packed = jnp.where(lane == c, flag, packed)
    out_ref[2 * COMP] = packed.astype(jnp.bfloat16)


def pack_own_kernel(spectra_hbm, mask_hbm, table_hbm, out_ref, table_ref, spectra_ref, mask_ref, sem):
    copies = [
        pltpu.make_async_copy(spectra_hbm, spectra_ref, sem.at[0]),
        pltpu.make_async_copy(mask_hbm, mask_ref, sem.at[1]),
    ] + [
        pltpu.make_async_copy(table_hbm.at[i, pl.ds(LAGS * j, LAGS)], table_ref.at[i, pl.ds(LAGS * j, LAGS)], sem.at[2 + 2 * i + j])
        for i in range(2)
        for j in range(2)
    ]
    for copy in copies:
        copy.start()
    for copy in copies:
        copy.wait()
    pack_into(out_ref, spectra_ref[...], mask_ref[...])


def pack_own(spectra, valid_mask, table):
    shape = (PLANES, spectra.shape[0], BINS)
    return pl.pallas_call(
        pack_own_kernel,
        out_shape=(jax.ShapeDtypeStruct(shape, jnp.bfloat16), jax.ShapeDtypeStruct(table.shape, table.dtype)),
        in_specs=[pl.BlockSpec(memory_space=pltpu.HBM)] * 3,
        out_specs=(pl.BlockSpec(memory_space=pltpu.VMEM), pl.BlockSpec(memory_space=pltpu.VMEM)),
        scratch_shapes=[
            pltpu.VMEM(spectra.shape, spectra.dtype),
            pltpu.VMEM(valid_mask.shape, valid_mask.dtype),
            pltpu.SemaphoreType.DMA((6,)),
        ],
        compiler_params=pltpu.CompilerParams(vmem_limit_bytes=1 << 20),
        name="pack_own",
    )(in_hbm(spectra), in_hbm(valid_mask), in_hbm(table))


def pack_two_kernel(own_ref, spectra_ref, mask_ref, out_ref):
    me = lax.axis_index("sub")
    out_ref[me] = own_ref[...]
    pack_into(out_ref.at[1 - me], spectra_ref[...], mask_ref[...])


def pack_two(own, spectra, valid_mask):
    return pl.pallas_call(
        pack_two_kernel,
        out_shape=jax.ShapeDtypeStruct((2, *own.shape), own.dtype),
        in_specs=[pl.BlockSpec(memory_space=pltpu.VMEM)] * 3,
        out_specs=pl.BlockSpec(memory_space=pltpu.VMEM),
        compiler_params=pltpu.CompilerParams(vmem_limit_bytes=1 << 20),
        name="pack_two",
    )(own, spectra, valid_mask)


def split(value):
    high = value.astype(jnp.bfloat16)
    return high, (value - high.astype(jnp.float32)).astype(jnp.bfloat16)


def dot_nt(left, right):
    return lax.dot_general(left, right, (((1,), (1,)), ((), ())), preferred_element_type=jnp.float32)


def shared_sums(left, right):
    total = None
    for one, other in zip(left, right):
        for i in range(len(one)):
            for j in range(len(other)):
                term = dot_nt(one[i], other[j])
                total = term if total is None else total + term
    return total / (2.0 * BINS)


def pair_kernel(chip_ref, *refs):
    moved_refs, (table_ref, out_ref, scr, x_scr, y_scr) = refs[:4], refs[4:]
    n_cs = n_row = 4
    shard = scr.shape[2]
    sub = lax.axis_index("sub")
    me_cs = lax.axis_index("col") * 2 + sub
    me_row = lax.axis_index("row")
    me = me_row * 4 + me_cs
    own = chip_ref[sub].astype(jnp.float32)
    scr[me_row] = own
    scr[4 + me_cs] = own
    scr[4 + (me_cs ^ 1)] = chip_ref[1 - sub].astype(jnp.float32)
    codes = arrival_codes()
    for j in range(4):
        code = sum(jnp.where(me == i, codes[i][j], 0) for i in range(N_PART))
        for t in range(2):
            scr[(code >> (4 * t)) & 15] = moved_refs[j][t].astype(jnp.float32)
    col_scr, row_scr = scr.at[:4], scr.at[4:8]
    rows, cols = n_cs * shard, n_row * shard
    per = 128 // cols
    col_planes = [jnp.concatenate([col_scr[j, q] for j in range(n_row)], axis=0) for q in range(PLANES)]
    for a in range(rows):
        x, y = None, None
        for c in range(COMP):
            re = row_scr[a // shard, 2 * c, pl.ds(a % shard, 1), :]
            im = row_scr[a // shard, 2 * c + 1, pl.ds(a % shard, 1), :]
            xc = re * col_planes[2 * c] + im * col_planes[2 * c + 1]
            yc = im * col_planes[2 * c] - re * col_planes[2 * c + 1]
            x = xc if x is None else x + xc
            y = yc if y is None else y + yc
        place = (a // per * per + (per - a % per) % per) * cols
        x_scr[pl.ds(place, cols), :] = x
        y_scr[pl.ds(place, cols), :] = y
    halves = []
    for scr, i in ((x_scr, 0), (y_scr, 1)):
        high, low = split(scr[...])
        first = dot_nt(table_ref[i], high)
        second = dot_nt(table_ref[i, :LAGS], low)
        halves.append(first[:LAGS] + first[LAGS:] + second)
    best = jnp.max(halves[0] + jnp.abs(halves[1]), axis=0, keepdims=True)
    pieces = []
    for h in range(rows // per):
        piece = jnp.broadcast_to(best[:, 128 * h : 128 * (h + 1)], (per, 128))
        pieces.append(pltpu.roll(piece, 0, 1, stride=cols, stride_axis=0)[:, :cols])
    peak = jnp.concatenate(pieces, axis=0) / (2.0 * BINS)
    row_planes = [jnp.concatenate([row_scr[j, q] for j in range(n_cs)], axis=0) for q in range(PLANES)]

    def energy(planes):
        return [split(planes[2 * c] * planes[2 * c] + planes[2 * c + 1] * planes[2 * c + 1]) for c in range(COMP)]

    def flags(planes):
        packed = planes[2 * COMP]
        return [(jnp.broadcast_to(packed[:, c : c + 1], packed.shape).astype(jnp.bfloat16),) for c in range(COMP)]

    shared_row = shared_sums(energy(row_planes), flags(col_planes))
    shared_col = shared_sums(flags(row_planes), energy(col_planes))
    out_ref[0] = peak / jnp.sqrt(jnp.maximum(shared_row * shared_col, FLOOR))


def arrival_codes():
    from_chip = []
    for legs in (LEG_A, LEG_B):
        source = {target: i for i, target in enumerate(legs)}
        from_chip.append([source[i] // 2 for i in range(N_PART)])
    codes = []
    for i in range(N_PART):
        arrivals = [from_chip[1][i], from_chip[0][i], from_chip[1][i ^ 1], from_chip[0][i ^ 1]]
        one = []
        for chip in arrivals:
            slots = []
            for t in range(2):
                if chip // 2 == i // 4:
                    slots.append(4 + (chip % 2) * 2 + t)
                else:
                    slots.append(chip // 2 if t == i % 2 else 8)
            one.append(slots[0] + 16 * slots[1])
        codes.append(one)
    return codes


def swap(value):
    return lax.ppermute(value, "sub", [(0, 1), (1, 0)])


def leg(value, targets):
    return lax.ppermute(value, ("row", "col", "sub"), list(enumerate(targets)))


def shards_small(spectra, valid_mask):
    shard = spectra.shape[0]
    sub_spectra, sub_mask = swap(spectra), swap(valid_mask)
    own, table = pack_own(spectra, valid_mask, jnp.asarray(phase_tables()))
    chip = pack_two(own, sub_spectra, sub_mask)
    leg_a, leg_b = leg(chip, LEG_A), leg(chip, LEG_B)
    swap_a, swap_b = swap(leg_a), swap(leg_b)
    rows = cols = 4 * shard
    return pl.pallas_call(
        pair_kernel,
        out_shape=jax.ShapeDtypeStruct((1, rows, cols), jnp.float32),
        scratch_shapes=[
            pltpu.VMEM((9, PLANES, shard, BINS), jnp.float32),
            pltpu.VMEM((rows * cols, BINS), jnp.float32),
            pltpu.VMEM((rows * cols, BINS), jnp.float32),
        ],
        in_specs=[pl.BlockSpec(memory_space=pltpu.VMEM)] * 6,
        out_specs=pl.BlockSpec(memory_space=pltpu.VMEM),
        compiler_params=pltpu.CompilerParams(vmem_limit_bytes=8 << 20),
        name="pairs",
    )(chip, leg_b, leg_a, swap_b, swap_a, table)


def shards_large(spectra, valid_mask):
    def planes(axes):
        records = lax.all_gather(spectra, axes, axis=0, tiled=True)
        flags = lax.all_gather(valid_mask, axes, axis=0, tiled=True)
        masked = (records * flags.astype(jnp.bfloat16)[:, :, None, None]).astype(jnp.float32)
        return masked, jnp.mean(masked * masked, axis=(2, 3)), flags.astype(jnp.float32)

    row, row_energy, row_flags = planes(("col", "sub"))
    col, col_energy, col_flags = planes("row")
    table = phase_tables().astype(np.float32)
    cosine, sine = table[:, : MAXLAG + 1] + table[:, LAGS : LAGS + MAXLAG + 1]

    def one(args):
        row_one, energy_one, flags_one = args
        re, im = row_one[None, :, 0], row_one[None, :, 1]
        x = jnp.sum(re * col[:, :, 0] + im * col[:, :, 1], axis=1)
        y = jnp.sum(im * col[:, :, 0] - re * col[:, :, 1], axis=1)
        even = jnp.dot(x, cosine.T, precision=lax.Precision.HIGHEST)
        odd = jnp.dot(y, sine.T, precision=lax.Precision.HIGHEST)
        peak = jnp.max(even + jnp.abs(odd), axis=1) / (2.0 * BINS)
        shared_row = jnp.sum((energy_one * flags_one)[None] * col_flags, axis=1)
        shared_col = jnp.sum(flags_one[None] * (col_energy * col_flags), axis=1)
        return peak / jnp.sqrt(jnp.maximum(shared_row * shared_col, FLOOR))

    return lax.map(one, (row, row_energy, row_flags))[None]


def solution(mesh):
    small = mesh.shape["row"] == 4 and mesh.shape["col"] == 2 and mesh.shape["sub"] == 2
    in_specs = (
        P(("grp", "row", "col", "sub"), None, None, None),
        P(("grp", "row", "col", "sub"), None),
    )
    out_specs = P(("col", "sub"), ("grp", "row"), None)
    return jax.shard_map(
        shards_small if small else shards_large, mesh=mesh, in_specs=in_specs, out_specs=out_specs, check_vma=False
    )
```

```python
import math

import jax
import jax.numpy as jnp
import numpy as np
from jax import lax
from jax.experimental import pallas as pl
from jax.experimental.pallas import tpu as pltpu
from jax.sharding import PartitionSpec as P

BINS = 256
COMP = 3
NSAMP = 2048
FIRST_BIN = 20
MAXLAG = 32
FLOOR = 0.25
N_PART = 16
LEG_A = (3, 5, 0, 11, 6, 8, 10, 15, 13, 4, 14, 2, 9, 1, 12, 7)
LEG_B = (9, 13, 6, 15, 12, 0, 4, 3, 11, 1, 8, 7, 14, 5, 10, 2)
PLANES = 2 * COMP + 1
LAGS = 40


def phase_tables():
    lag = np.arange(LAGS)
    lag = np.where(lag <= MAXLAG, lag, 0)
    angle = 2.0 * math.pi / NSAMP * lag[:, None] * (FIRST_BIN + np.arange(BINS))[None, :]
    both = []
    for table in (np.cos(angle), np.sin(angle)):
        high = table.astype(jnp.bfloat16)
        low = (table - high.astype(np.float64)).astype(jnp.bfloat16)
        both.append(np.concatenate([high, low], axis=0))
    return np.stack(both)


def in_hbm(value):
    return pltpu.with_memory_space_constraint(value, pltpu.HBM)


def pack_into(out_ref, records, flags):
    floats = records.astype(jnp.float32)
    flags = flags.astype(jnp.float32)
    lane = lax.broadcasted_iota(jnp.int32, (flags.shape[0], BINS), 1)
    packed = jnp.zeros(lane.shape, jnp.float32)
    for c in range(COMP):
        flag = jnp.broadcast_to(flags[:, c : c + 1], lane.shape)
        out_ref[2 * c] = (floats[:, c, 0, :] * flag).astype(jnp.bfloat16)
        out_ref[2 * c + 1] = (floats[:, c, 1, :] * flag).astype(jnp.bfloat16)
        packed = jnp.where(lane == c, flag, packed)
    out_ref[2 * COMP] = packed.astype(jnp.bfloat16)


def pack_own_kernel(spectra_hbm, mask_hbm, table_hbm, out_ref, table_ref, spectra_ref, mask_ref, sem):
    copies = [
        pltpu.make_async_copy(spectra_hbm, spectra_ref, sem.at[0]),
        pltpu.make_async_copy(mask_hbm, mask_ref, sem.at[1]),
    ] + [
        pltpu.make_async_copy(table_hbm.at[i, pl.ds(LAGS * j, LAGS)], table_ref.at[i, pl.ds(LAGS * j, LAGS)], sem.at[2 + 2 * i + j])
        for i in range(2)
        for j in range(2)
    ]
    for copy in copies:
        copy.start()
    for copy in copies:
        copy.wait()
    pack_into(out_ref, spectra_ref[...], mask_ref[...])


def pack_own(spectra, valid_mask, table):
    shape = (PLANES, spectra.shape[0], BINS)
    return pl.pallas_call(
        pack_own_kernel,
        out_shape=(jax.ShapeDtypeStruct(shape, jnp.bfloat16), jax.ShapeDtypeStruct(table.shape, table.dtype)),
        in_specs=[pl.BlockSpec(memory_space=pltpu.HBM)] * 3,
        out_specs=(pl.BlockSpec(memory_space=pltpu.VMEM), pl.BlockSpec(memory_space=pltpu.VMEM)),
        scratch_shapes=[
            pltpu.VMEM(spectra.shape, spectra.dtype),
            pltpu.VMEM(valid_mask.shape, valid_mask.dtype),
            pltpu.SemaphoreType.DMA((6,)),
        ],
        compiler_params=pltpu.CompilerParams(vmem_limit_bytes=1 << 20),
        name="pack_own",
    )(in_hbm(spectra), in_hbm(valid_mask), in_hbm(table))


def pack_two_kernel(own_ref, spectra_ref, mask_ref, out_ref):
    me = lax.axis_index("sub")
    out_ref[me] = own_ref[...]
    pack_into(out_ref.at[1 - me], spectra_ref[...], mask_ref[...])


def pack_two(own, spectra, valid_mask):
    return pl.pallas_call(
        pack_two_kernel,
        out_shape=jax.ShapeDtypeStruct((2, *own.shape), own.dtype),
        in_specs=[pl.BlockSpec(memory_space=pltpu.VMEM)] * 3,
        out_specs=pl.BlockSpec(memory_space=pltpu.VMEM),
        compiler_params=pltpu.CompilerParams(vmem_limit_bytes=1 << 20),
        name="pack_two",
    )(own, spectra, valid_mask)


def split(value):
    high = value.astype(jnp.bfloat16)
    return high, (value - high.astype(jnp.float32)).astype(jnp.bfloat16)


def dot_nt(left, right):
    return lax.dot_general(left, right, (((1,), (1,)), ((), ())), preferred_element_type=jnp.float32)


def shared_sums(left, right):
    total = None
    for one, other in zip(left, right):
        for i in range(len(one)):
            for j in range(len(other)):
                term = dot_nt(one[i], other[j])
                total = term if total is None else total + term
    return total / (2.0 * BINS)


def of_device(table):
    me = lax.axis_index("row") * 4 + lax.axis_index("col") * 2 + lax.axis_index("sub")
    return sum(jnp.where(me == i, table[i], 0) for i in range(N_PART))


def put(scr, legs, first, ref):
    code = of_device(arrival_codes(legs, first))
    for t in range(2):
        scr[(code >> (4 * t)) & 15] = ref[t].astype(jnp.float32)


def place_kernel(chip_ref, b_ref, a_ref, scr):
    sub = lax.axis_index("sub")
    me_cs = lax.axis_index("col") * 2 + sub
    own = chip_ref[sub].astype(jnp.float32)
    scr[lax.axis_index("row")] = own
    scr[4 + me_cs] = own
    scr[4 + (me_cs ^ 1)] = chip_ref[1 - sub].astype(jnp.float32)
    put(scr, LEG_A, 0, a_ref)
    put(scr, LEG_B, 0, b_ref)


def place(chip, leg_b, leg_a):
    return pl.pallas_call(
        place_kernel,
        out_shape=jax.ShapeDtypeStruct((9, *chip.shape[1:]), jnp.float32),
        in_specs=[pl.BlockSpec(memory_space=pltpu.VMEM)] * 3,
        out_specs=pl.BlockSpec(memory_space=pltpu.VMEM),
        compiler_params=pltpu.CompilerParams(vmem_limit_bytes=1 << 20),
        cost_estimate=pl.CostEstimate(flops=1000000000, bytes_accessed=0, transcendentals=0),
        name="place",
    )(chip, leg_b, leg_a)


def pair_kernel(placed_ref, b_ref, a_ref, table_ref, out_ref, scr, x_scr, y_scr):
    n_cs = n_row = 4
    shard = scr.shape[2]
    put(scr, LEG_A, 1, a_ref)
    put(scr, LEG_B, 1, b_ref)
    col_scr, row_scr = scr.at[:4], scr.at[4:8]
    rows, cols = n_cs * shard, n_row * shard
    per = 128 // cols
    col_planes = [jnp.concatenate([col_scr[j, q] for j in range(n_row)], axis=0) for q in range(PLANES)]
    for a in range(rows):
        x, y = None, None
        for c in range(COMP):
            re = row_scr[a // shard, 2 * c, pl.ds(a % shard, 1), :]
            im = row_scr[a // shard, 2 * c + 1, pl.ds(a % shard, 1), :]
            xc = re * col_planes[2 * c] + im * col_planes[2 * c + 1]
            yc = im * col_planes[2 * c] - re * col_planes[2 * c + 1]
            x = xc if x is None else x + xc
            y = yc if y is None else y + yc
        place = (a // per * per + (per - a % per) % per) * cols
        x_scr[pl.ds(place, cols), :] = x
        y_scr[pl.ds(place, cols), :] = y
    halves = []
    for scr, i in ((x_scr, 0), (y_scr, 1)):
        high, low = split(scr[...])
        first = dot_nt(table_ref[i], high)
        second = dot_nt(table_ref[i, :LAGS], low)
        halves.append(first[:LAGS] + first[LAGS:] + second)
    best = jnp.max(halves[0] + jnp.abs(halves[1]), axis=0, keepdims=True)
    pieces = []
    for h in range(rows // per):
        piece = jnp.broadcast_to(best[:, 128 * h : 128 * (h + 1)], (per, 128))
        pieces.append(pltpu.roll(piece, 0, 1, stride=cols, stride_axis=0)[:, :cols])
    peak = jnp.concatenate(pieces, axis=0) / (2.0 * BINS)
    row_planes = [jnp.concatenate([row_scr[j, q] for j in range(n_cs)], axis=0) for q in range(PLANES)]

    def energy(planes):
        return [split(planes[2 * c] * planes[2 * c] + planes[2 * c + 1] * planes[2 * c + 1]) for c in range(COMP)]

    def flags(planes):
        packed = planes[2 * COMP]
        return [(jnp.broadcast_to(packed[:, c : c + 1], packed.shape).astype(jnp.bfloat16),) for c in range(COMP)]

    shared_row = shared_sums(energy(row_planes), flags(col_planes))
    shared_col = shared_sums(flags(row_planes), energy(col_planes))
    out_ref[0] = peak / jnp.sqrt(jnp.maximum(shared_row * shared_col, FLOOR))


def arrival_codes(legs, other):
    source = {target: i for i, target in enumerate(legs)}
    codes = []
    for i in range(N_PART):
        chip = source[i ^ other] // 2
        if chip // 2 == i // 4:
            slots = [4 + (chip % 2) * 2, 5 + (chip % 2) * 2]
        else:
            slots = [chip // 2 if t == i % 2 else 8 for t in range(2)]
        codes.append(slots[0] + 16 * slots[1])
    return codes


def swap(value):
    return lax.ppermute(value, "sub", [(0, 1), (1, 0)])


def leg(value, targets):
    return lax.ppermute(value, ("row", "col", "sub"), list(enumerate(targets)))


def shards_small(spectra, valid_mask):
    shard = spectra.shape[0]
    sub_spectra, sub_mask = swap(spectra), swap(valid_mask)
    own, table = pack_own(spectra, valid_mask, jnp.asarray(phase_tables()))
    chip = pack_two(own, sub_spectra, sub_mask)
    leg_a, leg_b = leg(chip, LEG_A), leg(chip, LEG_B)
    swap_a, swap_b = swap(leg_a), swap(leg_b)
    placed = place(chip, leg_b, leg_a)
    rows = cols = 4 * shard
    return pl.pallas_call(
        pair_kernel,
        out_shape=(jax.ShapeDtypeStruct((1, rows, cols), jnp.float32), jax.ShapeDtypeStruct(placed.shape, placed.dtype)),
        scratch_shapes=[
            pltpu.VMEM((rows * cols, BINS), jnp.float32),
            pltpu.VMEM((rows * cols, BINS), jnp.float32),
        ],
        in_specs=[pl.BlockSpec(memory_space=pltpu.VMEM)] * 4,
        out_specs=(pl.BlockSpec(memory_space=pltpu.VMEM), pl.BlockSpec(memory_space=pltpu.VMEM)),
        input_output_aliases={0: 1},
        compiler_params=pltpu.CompilerParams(vmem_limit_bytes=8 << 20),
        name="pairs",
    )(placed, swap_b, swap_a, table)[0]


def shards_large(spectra, valid_mask):
    def planes(axes):
        records = lax.all_gather(spectra, axes, axis=0, tiled=True)
        flags = lax.all_gather(valid_mask, axes, axis=0, tiled=True)
        masked = (records * flags.astype(jnp.bfloat16)[:, :, None, None]).astype(jnp.float32)
        return masked, jnp.mean(masked * masked, axis=(2, 3)), flags.astype(jnp.float32)

    row, row_energy, row_flags = planes(("col", "sub"))
    col, col_energy, col_flags = planes("row")
    table = phase_tables().astype(np.float32)
    cosine, sine = table[:, : MAXLAG + 1] + table[:, LAGS : LAGS + MAXLAG + 1]

    def one(args):
        row_one, energy_one, flags_one = args
        re, im = row_one[None, :, 0], row_one[None, :, 1]
        x = jnp.sum(re * col[:, :, 0] + im * col[:, :, 1], axis=1)
        y = jnp.sum(im * col[:, :, 0] - re * col[:, :, 1], axis=1)
        even = jnp.dot(x, cosine.T, precision=lax.Precision.HIGHEST)
        odd = jnp.dot(y, sine.T, precision=lax.Precision.HIGHEST)
        peak = jnp.max(even + jnp.abs(odd), axis=1) / (2.0 * BINS)
        shared_row = jnp.sum((energy_one * flags_one)[None] * col_flags, axis=1)
        shared_col = jnp.sum(flags_one[None] * (col_energy * col_flags), axis=1)
        return peak / jnp.sqrt(jnp.maximum(shared_row * shared_col, FLOOR))

    return lax.map(one, (row, row_energy, row_flags))[None]


def solution(mesh):
    small = mesh.shape["row"] == 4 and mesh.shape["col"] == 2 and mesh.shape["sub"] == 2
    in_specs = (
        P(("grp", "row", "col", "sub"), None, None, None),
        P(("grp", "row", "col", "sub"), None),
    )
    out_specs = P(("col", "sub"), ("grp", "row"), None)
    return jax.shard_map(
        shards_small if small else shards_large, mesh=mesh, in_specs=in_specs, out_specs=out_specs, check_vma=False
    )
```

```python
import math

import jax
import jax.numpy as jnp
import numpy as np
from jax import lax
from jax.experimental import pallas as pl
from jax.experimental.pallas import tpu as pltpu
from jax.sharding import PartitionSpec as P

BINS = 256
COMP = 3
NSAMP = 2048
FIRST_BIN = 20
MAXLAG = 32
FLOOR = 0.25
N_PART = 16
LEG_A = (2, 5, 7, 0, 13, 9, 11, 14, 12, 4, 3, 8, 15, 1, 10, 6)
LEG_B = (9, 13, 15, 10, 6, 0, 2, 4, 11, 1, 7, 14, 5, 8, 12, 3)
PLANES = 2 * COMP + 1
LAGS = 40


def phase_tables():
    lag = np.arange(LAGS)
    lag = np.where(lag <= MAXLAG, lag, 0)
    angle = 2.0 * math.pi / NSAMP * lag[:, None] * (FIRST_BIN + np.arange(BINS))[None, :]
    both = []
    for table in (np.cos(angle), np.sin(angle)):
        high = table.astype(jnp.bfloat16)
        low = (table - high.astype(np.float64)).astype(jnp.bfloat16)
        both.append(np.concatenate([high, low], axis=0))
    return np.stack(both)


def in_hbm(value):
    return pltpu.with_memory_space_constraint(value, pltpu.HBM)


def pack_into(out_ref, records, flags):
    floats = records.astype(jnp.float32)
    flags = flags.astype(jnp.float32)
    lane = lax.broadcasted_iota(jnp.int32, (flags.shape[0], BINS), 1)
    packed = jnp.zeros(lane.shape, jnp.float32)
    for c in range(COMP):
        flag = jnp.broadcast_to(flags[:, c : c + 1], lane.shape)
        out_ref[2 * c] = (floats[:, c, 0, :] * flag).astype(jnp.bfloat16)
        out_ref[2 * c + 1] = (floats[:, c, 1, :] * flag).astype(jnp.bfloat16)
        packed = jnp.where(lane == c, flag, packed)
    out_ref[2 * COMP] = packed.astype(jnp.bfloat16)


def pack_own_kernel(spectra_hbm, mask_hbm, table_hbm, out_ref, table_ref, spectra_ref, mask_ref, sem):
    copies = [
        pltpu.make_async_copy(spectra_hbm, spectra_ref, sem.at[0]),
        pltpu.make_async_copy(mask_hbm, mask_ref, sem.at[1]),
    ] + [
        pltpu.make_async_copy(table_hbm.at[i, pl.ds(LAGS * j, LAGS)], table_ref.at[i, pl.ds(LAGS * j, LAGS)], sem.at[2 + 2 * i + j])
        for i in range(2)
        for j in range(2)
    ]
    for copy in copies:
        copy.start()
    for copy in copies:
        copy.wait()
    pack_into(out_ref, spectra_ref[...], mask_ref[...])


def pack_own(spectra, valid_mask, table):
    shape = (PLANES, spectra.shape[0], BINS)
    return pl.pallas_call(
        pack_own_kernel,
        out_shape=(jax.ShapeDtypeStruct(shape, jnp.bfloat16), jax.ShapeDtypeStruct(table.shape, table.dtype)),
        in_specs=[pl.BlockSpec(memory_space=pltpu.HBM)] * 3,
        out_specs=(pl.BlockSpec(memory_space=pltpu.VMEM), pl.BlockSpec(memory_space=pltpu.VMEM)),
        scratch_shapes=[
            pltpu.VMEM(spectra.shape, spectra.dtype),
            pltpu.VMEM(valid_mask.shape, valid_mask.dtype),
            pltpu.SemaphoreType.DMA((6,)),
        ],
        compiler_params=pltpu.CompilerParams(vmem_limit_bytes=1 << 20),
        name="pack_own",
    )(in_hbm(spectra), in_hbm(valid_mask), in_hbm(table))


def pack_two_kernel(own_ref, spectra_ref, mask_ref, out_ref):
    me = lax.axis_index("sub")
    out_ref[me] = own_ref[...]
    pack_into(out_ref.at[1 - me], spectra_ref[...], mask_ref[...])


def pack_two(own, spectra, valid_mask):
    return pl.pallas_call(
        pack_two_kernel,
        out_shape=jax.ShapeDtypeStruct((2, *own.shape), own.dtype),
        in_specs=[pl.BlockSpec(memory_space=pltpu.VMEM)] * 3,
        out_specs=pl.BlockSpec(memory_space=pltpu.VMEM),
        compiler_params=pltpu.CompilerParams(vmem_limit_bytes=1 << 20),
        name="pack_two",
    )(own, spectra, valid_mask)


def split(value):
    high = value.astype(jnp.bfloat16)
    return high, (value - high.astype(jnp.float32)).astype(jnp.bfloat16)


def dot_nt(left, right):
    return lax.dot_general(left, right, (((1,), (1,)), ((), ())), preferred_element_type=jnp.float32)


def shared_sums(left, right):
    total = None
    for one, other in zip(left, right):
        for i in range(len(one)):
            for j in range(len(other)):
                term = dot_nt(one[i], other[j])
                total = term if total is None else total + term
    return total / (2.0 * BINS)


def of_device(table):
    me = lax.axis_index("row") * 4 + lax.axis_index("col") * 2 + lax.axis_index("sub")
    return sum(jnp.where(me == i, table[i], 0) for i in range(N_PART))


def put(scr, legs, first, ref):
    code = of_device(arrival_codes(legs, first))
    for t in range(2):
        scr[(code >> (4 * t)) & 15] = ref[t].astype(jnp.float32)


def place_kernel(chip_ref, b_ref, a_ref, scr):
    sub = lax.axis_index("sub")
    me_cs = lax.axis_index("col") * 2 + sub
    own = chip_ref[sub].astype(jnp.float32)
    scr[lax.axis_index("row")] = own
    scr[4 + me_cs] = own
    scr[4 + (me_cs ^ 1)] = chip_ref[1 - sub].astype(jnp.float32)
    put(scr, LEG_A, 0, a_ref)
    put(scr, LEG_B, 0, b_ref)


def place(chip, leg_b, leg_a):
    return pl.pallas_call(
        place_kernel,
        out_shape=jax.ShapeDtypeStruct((9, *chip.shape[1:]), jnp.float32),
        in_specs=[pl.BlockSpec(memory_space=pltpu.VMEM)] * 3,
        out_specs=pl.BlockSpec(memory_space=pltpu.VMEM),
        compiler_params=pltpu.CompilerParams(vmem_limit_bytes=1 << 20),
        cost_estimate=pl.CostEstimate(flops=1000000000, bytes_accessed=0, transcendentals=0),
        name="place",
    )(chip, leg_b, leg_a)


def pair_kernel(placed_ref, b_ref, a_ref, table_ref, out_ref, scr, x_scr, y_scr):
    n_cs = n_row = 4
    shard = scr.shape[2]
    put(scr, LEG_A, 1, a_ref)
    put(scr, LEG_B, 1, b_ref)
    col_scr, row_scr = scr.at[:4], scr.at[4:8]
    rows, cols = n_cs * shard, n_row * shard
    per = 128 // cols
    col_planes = [jnp.concatenate([col_scr[j, q] for j in range(n_row)], axis=0) for q in range(PLANES)]
    for a in range(rows):
        x, y = None, None
        for c in range(COMP):
            re = row_scr[a // shard, 2 * c, pl.ds(a % shard, 1), :]
            im = row_scr[a // shard, 2 * c + 1, pl.ds(a % shard, 1), :]
            xc = re * col_planes[2 * c] + im * col_planes[2 * c + 1]
            yc = im * col_planes[2 * c] - re * col_planes[2 * c + 1]
            x = xc if x is None else x + xc
            y = yc if y is None else y + yc
        place = (a // per * per + (per - a % per) % per) * cols
        x_scr[pl.ds(place, cols), :] = x
        y_scr[pl.ds(place, cols), :] = y
    halves = []
    for scr, i in ((x_scr, 0), (y_scr, 1)):
        high, low = split(scr[...])
        first = dot_nt(table_ref[i], high)
        second = dot_nt(table_ref[i, :LAGS], low)
        halves.append(first[:LAGS] + first[LAGS:] + second)
    best = jnp.max(halves[0] + jnp.abs(halves[1]), axis=0, keepdims=True)
    pieces = []
    for h in range(rows // per):
        piece = jnp.broadcast_to(best[:, 128 * h : 128 * (h + 1)], (per, 128))
        pieces.append(pltpu.roll(piece, 0, 1, stride=cols, stride_axis=0)[:, :cols])
    peak = jnp.concatenate(pieces, axis=0) / (2.0 * BINS)
    row_planes = [jnp.concatenate([row_scr[j, q] for j in range(n_cs)], axis=0) for q in range(PLANES)]

    def energy(planes):
        return [split(planes[2 * c] * planes[2 * c] + planes[2 * c + 1] * planes[2 * c + 1]) for c in range(COMP)]

    def flags(planes):
        packed = planes[2 * COMP]
        return [(jnp.broadcast_to(packed[:, c : c + 1], packed.shape).astype(jnp.bfloat16),) for c in range(COMP)]

    shared_row = shared_sums(energy(row_planes), flags(col_planes))
    shared_col = shared_sums(flags(row_planes), energy(col_planes))
    out_ref[0] = peak / jnp.sqrt(jnp.maximum(shared_row * shared_col, FLOOR))


def arrival_codes(legs, other):
    source = {target: i for i, target in enumerate(legs)}
    codes = []
    for i in range(N_PART):
        chip = source[i ^ other] // 2
        if chip // 2 == i // 4:
            slots = [4 + (chip % 2) * 2, 5 + (chip % 2) * 2]
        else:
            slots = [chip // 2 if t == i % 2 else 8 for t in range(2)]
        codes.append(slots[0] + 16 * slots[1])
    return codes


def swap(value):
    return lax.ppermute(value, "sub", [(0, 1), (1, 0)])


def leg(value, targets):
    return lax.ppermute(value, ("row", "col", "sub"), list(enumerate(targets)))


def shards_small(spectra, valid_mask):
    shard = spectra.shape[0]
    sub_spectra, sub_mask = swap(spectra), swap(valid_mask)
    own, table = pack_own(spectra, valid_mask, jnp.asarray(phase_tables()))
    chip = pack_two(own, sub_spectra, sub_mask)
    leg_a, leg_b = leg(chip, LEG_A), leg(chip, LEG_B)
    swap_a, swap_b = swap(leg_a), swap(leg_b)
    placed = place(chip, leg_b, leg_a)
    rows = cols = 4 * shard
    return pl.pallas_call(
        pair_kernel,
        out_shape=(jax.ShapeDtypeStruct((1, rows, cols), jnp.float32), jax.ShapeDtypeStruct(placed.shape, placed.dtype)),
        scratch_shapes=[
            pltpu.VMEM((rows * cols, BINS), jnp.float32),
            pltpu.VMEM((rows * cols, BINS), jnp.float32),
        ],
        in_specs=[pl.BlockSpec(memory_space=pltpu.VMEM)] * 4,
        out_specs=(pl.BlockSpec(memory_space=pltpu.VMEM), pl.BlockSpec(memory_space=pltpu.VMEM)),
        input_output_aliases={0: 1},
        compiler_params=pltpu.CompilerParams(vmem_limit_bytes=8 << 20),
        name="pairs",
    )(placed, swap_b, swap_a, table)[0]


def shards_large(spectra, valid_mask):
    def planes(axes):
        records = lax.all_gather(spectra, axes, axis=0, tiled=True)
        flags = lax.all_gather(valid_mask, axes, axis=0, tiled=True)
        masked = (records * flags.astype(jnp.bfloat16)[:, :, None, None]).astype(jnp.float32)
        return masked, jnp.mean(masked * masked, axis=(2, 3)), flags.astype(jnp.float32)

    row, row_energy, row_flags = planes(("col", "sub"))
    col, col_energy, col_flags = planes("row")
    table = phase_tables().astype(np.float32)
    cosine, sine = table[:, : MAXLAG + 1] + table[:, LAGS : LAGS + MAXLAG + 1]

    def one(args):
        row_one, energy_one, flags_one = args
        re, im = row_one[None, :, 0], row_one[None, :, 1]
        x = jnp.sum(re * col[:, :, 0] + im * col[:, :, 1], axis=1)
        y = jnp.sum(im * col[:, :, 0] - re * col[:, :, 1], axis=1)
        even = jnp.dot(x, cosine.T, precision=lax.Precision.HIGHEST)
        odd = jnp.dot(y, sine.T, precision=lax.Precision.HIGHEST)
        peak = jnp.max(even + jnp.abs(odd), axis=1) / (2.0 * BINS)
        shared_row = jnp.sum((energy_one * flags_one)[None] * col_flags, axis=1)
        shared_col = jnp.sum(flags_one[None] * (col_energy * col_flags), axis=1)
        return peak / jnp.sqrt(jnp.maximum(shared_row * shared_col, FLOOR))

    return lax.map(one, (row, row_energy, row_flags))[None]


def solution(mesh):
    small = mesh.shape["row"] == 4 and mesh.shape["col"] == 2 and mesh.shape["sub"] == 2
    in_specs = (
        P(("grp", "row", "col", "sub"), None, None, None),
        P(("grp", "row", "col", "sub"), None),
    )
    out_specs = P(("col", "sub"), ("grp", "row"), None)
    return jax.shard_map(
        shards_small if small else shards_large, mesh=mesh, in_specs=in_specs, out_specs=out_specs, check_vma=False
    )
```
